32 devices in a mesh: grp: 2 (over x), ka: 16 (over z, y, core).
Axes of the slice: x: 2, y: 2, z: 4, core: 2. Of those that a mesh axis runs over, the one named last changes fastest.
Arguments:
- amplitudes: bfloat16 [2, 16, 2, 2, 64, 64], P('grp', 'ka'), may hold values from -6 to 6
- valence_orbitals: bfloat16 [16, 2, 64, 384], P('ka'), may hold values from -0.75 to 0.75
- conduction_orbitals: bfloat16 [16, 2, 64, 384], P('ka'), may hold values from -0.75 to 0.75
- screened: float32 [2, 16, 147456], P(None, None, 'ka'), may hold values from -0.25 to 0.25
- coupling: float32 [2, 16, 147456], P(None, None, 'ka'), may hold values from -0.1875 to 0.1875
- grid_index: int32 [16], replicated, may hold values from 0 to 15, each once
- valence_index: int32 [16, 64], P('ka'), may hold values from 0 to 255
- conduction_index: int32 [16, 64], P('ka'), may hold values from 0 to 255
- valence_table: float32 [256], replicated, may hold values from -2 to -0.2
- conduction_table: float32 [256], replicated, may hold values from 0.2 to 2
Outputs:
- action: bfloat16 [2, 16, 2, 2, 64, 64], P('grp', 'ka')
The draws below stay inside these ranges and needn't reach their ends.
Inputs may be any that keep to these rules, and one draw needn't show every extreme that they name: `grid_index`: each of 0 to 15 appears once.
All inputs are finite; a program needn't handle non-finite values.
Results may differ from the reference program's by a relative error of at most 0.014.
Values may be sent and summed in bfloat16 or wider, within the bound.
A program may use at most 192 MiB of HBM per device.

```python
import jax
import jax.numpy as jnp
from jax import lax

NV = 64
NC = 64
NMU = 384
NTAB = 256
NVEC = 2
K = 16
PAIRS = 147456


def set_ends(values, stream_key, low, top_value):
    shape = values.shape
    place = [jax.random.randint(jax.random.fold_in(stream_key, axis), (), 0, shape[axis]) for axis in range(len(shape))]
    values = values.at[tuple(place)].set(low)
    longest = shape.index(max(shape))
    place[longest] = (place[longest] + 1) % shape[longest]
    return values.at[tuple(place)].set(top_value)


def levels(own_key, shape, cuts, least, top_value):
    def one(position, shards_of):
        steps = jax.random.uniform(jax.random.fold_in(jax.random.fold_in(own_key, 6), position), (shards_of,), jnp.float32, least / len(cuts), top_value / len(cuts))
        return jnp.repeat(jnp.exp(steps), shape[position] // shards_of).reshape((-1,) + (1,) * (len(shape) - position - 1))

    factor_of = one(*cuts[0])
    for cut in cuts[1:]:
        factor_of = factor_of * one(*cut)
    return factor_of


def normal_values(stream_key, shape, width, most, cuts=(), kind=jnp.bfloat16):
    array = jax.random.normal(stream_key, shape, jnp.float32) * width
    if len(cuts) > 0:
        array = levels(stream_key, shape, cuts, -0.22, 0.18) * array
    return jnp.clip(array, min=-most, max=most).astype(kind)


def setup_inputs(seed: int = 0) -> dict:
    streams_of = jax.random.split(jax.random.key(seed), 11)
    return {
        "amplitudes": normal_values(streams_of[0], (2, K, 2, NVEC, NV, NC), 1.0, 6.0, ((0, 2), (1, 16))),
        "valence_orbitals": normal_values(streams_of[1], (K, 2, NV, NMU), NV ** -0.5, 0.75, ((0, 16),)),
        "conduction_orbitals": normal_values(streams_of[2], (K, 2, NC, NMU), NC ** -0.5, 0.75, ((0, 16),)),
        "screened": normal_values(streams_of[3], (2, K, PAIRS), 0.04, 0.25, ((2, 16),), jnp.float32),
        "coupling": normal_values(streams_of[4], (2, K, PAIRS), 0.03, 0.1875, ((2, 16),), jnp.float32),
        "grid_index": jax.random.permutation(streams_of[5], K).astype(jnp.int32),
        "valence_index": set_ends(jax.random.randint(streams_of[6], (K, NV), 0, NTAB), jax.random.fold_in(streams_of[6], 1), 0, NTAB - 1).astype(jnp.int32),
        "conduction_index": set_ends(jax.random.randint(streams_of[7], (K, NC), 0, NTAB), jax.random.fold_in(streams_of[7], 1), 0, NTAB - 1).astype(jnp.int32),
        "valence_table": jnp.clip(jax.random.uniform(streams_of[8], (NTAB,), jnp.float32, -2.0, -0.2), -2.0, -0.2),
        "conduction_table": jnp.clip(jax.random.uniform(streams_of[9], (NTAB,), jnp.float32, 0.2, 2.0), 0.2, 2.0),
    }


precise = lax.Precision.HIGHEST


def lattice_tables(grid_index):
    points = grid_index.shape[0]
    grid_side = points // 4
    lattice = jnp.arange(points, dtype=jnp.int32)
    turn_count = (lattice[:, None] // grid_side) * (grid_index[None, :] // grid_side) * grid_side
    turn_count = turn_count + 4 * (lattice[:, None] % grid_side) * (grid_index[None, :] % grid_side)
    turn_count = turn_count % points
    phases = turn_count.astype(jnp.float32) * (2.0 * jnp.pi / points)
    return jnp.cos(phases), -jnp.sin(phases)


def rounded(values):
    return lax.optimization_barrier(values.astype(jnp.bfloat16))


def product(formula, left_side, right_side):
    return jnp.einsum(formula, left_side.astype(jnp.float32), right_side.astype(jnp.float32), precision=precise)


def complex_product(formula, left_real, left_imag, right_real, right_imag):
    real_part = product(formula, left_real, right_real) - product(formula, left_imag, right_imag)
    imag_part = product(formula, left_real, right_imag) + product(formula, left_imag, right_real)
    return real_part, imag_part


def apply_table(table_real, table_imag, data_real, data_imag):
    real_part = jnp.dot(table_real, data_real, precision=precise) - jnp.dot(table_imag, data_imag, precision=precise)
    imag_part = jnp.dot(table_real, data_imag, precision=precise) + jnp.dot(table_imag, data_real, precision=precise)
    return real_part, imag_part


def interpolate(trial_vector, valence, conduction):
    half_real, half_imag = complex_product("kvc,kcn->kvn", trial_vector[:, 0], trial_vector[:, 1], conduction[:, 0], conduction[:, 1])
    half_real = rounded(half_real)
    half_imag = rounded(half_imag)
    pair_real, pair_imag = complex_product("kvm,kvn->kmn", valence[:, 0], valence[:, 1], half_real, half_imag)
    pair_real = rounded(pair_real).astype(jnp.float32).reshape(K, -1)
    pair_imag = rounded(pair_imag).astype(jnp.float32).reshape(K, -1)
    return pair_real, pair_imag


def project(back_real, back_imag, valence, conduction):
    grid_real = back_real.reshape(K, NMU, NMU)
    grid_imag = back_imag.reshape(K, NMU, NMU)
    proj_real, proj_imag = complex_product("kvm,kmn->kvn", valence[:, 0], valence[:, 1], grid_real, grid_imag)
    proj_real = rounded(proj_real)
    proj_imag = rounded(proj_imag)
    kern_real, kern_imag = complex_product("kvn,kcn->kvc", proj_real, proj_imag, conduction[:, 0], conduction[:, 1])
    return jnp.stack([kern_real, kern_imag], axis=1)


def reference(amplitudes, valence_orbitals, conduction_orbitals, screened, coupling, grid_index, valence_index, conduction_index, valence_table, conduction_table):
    forward_real, forward_imag = lattice_tables(grid_index)
    inverse_real = forward_real.T / K
    inverse_imag = -forward_imag.T / K
    energy = conduction_table[conduction_index][:, None, :] - valence_table[valence_index][:, :, None]

    def one_vector(trial_pair):
        spectra = []
        for group_id in range(2):
            pair_real, pair_imag = interpolate(trial_pair[group_id], valence_orbitals, conduction_orbitals)
            spectra.append(apply_table(forward_real, forward_imag, pair_real, pair_imag))
        results = []
        for group_id in range(2):
            own_real, own_imag = spectra[group_id]
            far_real, far_imag = spectra[1 - group_id]
            direct_real = screened[0] * own_real - screened[1] * own_imag
            direct_imag = screened[0] * own_imag + screened[1] * own_real
            cross_real = coupling[0] * far_real - coupling[1] * far_imag
            cross_imag = coupling[0] * far_imag + coupling[1] * far_real
            summed_real = direct_real + cross_real
            summed_imag = direct_imag + cross_imag
            back_real, back_imag = apply_table(inverse_real, inverse_imag, summed_real, summed_imag)
            kernel = project(rounded(back_real), rounded(back_imag), valence_orbitals, conduction_orbitals)
            sign_value = 1.0 - 2.0 * group_id
            result = sign_value * (energy[:, None] * trial_pair[group_id].astype(jnp.float32) - kernel)
            results.append(result.astype(jnp.bfloat16))
        return jnp.stack(results)

    stacked = lax.map(one_vector, jnp.moveaxis(amplitudes, 3, 0))
    return jnp.moveaxis(stacked, 0, 3)
```

```python
import functools

import jax
import jax.numpy as jnp
from jax import lax
from jax.experimental import pallas as pl
from jax.experimental.pallas import tpu as pltpu
from jax.sharding import PartitionSpec as P

F32 = jnp.float32
BF16 = jnp.bfloat16
precise = lax.Precision.HIGHEST


def lattice_tables(grid_index):
    points = grid_index.shape[0]
    grid_side = points // 4
    lattice = jnp.arange(points, dtype=jnp.int32)
    turn_count = lattice[:, None] // grid_side * (grid_index[None, :] // grid_side) * grid_side
    turn_count = turn_count + 4 * (lattice[:, None] % grid_side) * (grid_index[None, :] % grid_side)
    turn_count = turn_count % points
    phases = turn_count.astype(F32) * (2.0 * jnp.pi / points)
    return (jnp.cos(phases), -jnp.sin(phases))


def lookup(indices, table_values):
    levels = jnp.arange(table_values.shape[0], dtype=jnp.int32)
    onehot = (indices[..., None] == levels).astype(F32)
    return jnp.einsum("kvt,t->kv", onehot, table_values, precision=precise)


def swap_parts(values):
    half = values.shape[-1] // 2
    turned = pltpu.roll(values, half, values.ndim - 1)
    lanes = lax.broadcasted_iota(jnp.int32, values.shape, values.ndim - 1)
    return jnp.where(lanes < half, -turned, turned)


def middle_kernel(split, chunk, rows_b, fr_ref, fi_ref, b_ref, c_ref, screened_ref, coupling_ref, t_ref,
                  left, weight, spec, mixed, scr, cpl, sems):
    points = fr_ref.shape[0]
    nmu = c_ref.shape[2] // 2
    half_c = c_ref.shape[1]
    wide = 2 * half_c
    width = scr.shape[2]
    start = lax.axis_index("grp") * width if split > 1 else 0
    span = pl.ds(pl.multiple_of(start, 128), width)
    load_s = pltpu.make_async_copy(screened_ref.at[:, :, span], scr, sems.at[0])
    load_c = pltpu.make_async_copy(coupling_ref.at[:, :, span], cpl, sems.at[1])
    load_s.start()
    load_c.start()
    chunks = points // chunk
    rows = rows_b * points

    def fill(base):
        for i in range(chunk):
            block = c_ref[base + i]
            weight[i * wide : i * wide + half_c] = block
            weight[i * wide + half_c : (i + 1) * wide] = jnp.concatenate(
                [-block[:, nmu:], block[:, :nmu]], axis=1
            )

    def forward(step, carry):
        base = step * chunk
        fill(base)
        for group in range(2):
            for i in range(chunk):
                lanes = pl.ds(pl.multiple_of((base + i) * wide, 128), wide)
                data = b_ref[base + i, group].astype(F32)
                turned = swap_parts(data)
                table_r = fr_ref[:, lanes]
                table_i = fi_ref[:, lanes]
                block = table_r[None] * data[:, None, :] + table_i[None] * turned[:, None, :]
                left[:, i * wide : (i + 1) * wide] = block.reshape(rows, wide).astype(BF16)
            part = jnp.dot(left[...], weight[...], preferred_element_type=F32)

            @pl.when(step == 0)
            def _():
                spec[group] = part

            @pl.when(step > 0)
            def _():
                spec[group] += part

        return carry

    lax.fori_loop(0, chunks, forward, 0)
    load_s.wait()
    load_c.wait()

    def weigh(pos, carry):
        mu = pos // 2
        lanes = pl.ds(pl.multiple_of(mu * nmu, 128), nmu)
        at = pl.ds(pl.multiple_of(pos * points, points), points)
        sr, si = scr[0, :, lanes], scr[1, :, lanes]
        cr, ci = cpl[0, :, lanes], cpl[1, :, lanes]
        fields = [(spec[g, at, :nmu], spec[g, at, nmu:]) for g in range(2)]
        for g in range(2):
            (ar, ai), (br, bi) = fields[g], fields[1 - g]
            real = sr * ar - si * ai + cr * br - ci * bi
            imag = sr * ai + si * ar + cr * bi + ci * br
            mixed[g, at, :nmu] = real.astype(BF16)
            mixed[g, at, nmu:] = (-imag).astype(BF16)
        return carry

    lax.fori_loop(0, rows_b, weigh, 0)

    def backward(step, carry):
        base = step * chunk
        fill(base)
        for group in range(2):
            product = lax.dot_general(
                mixed[group], weight[...], (((1,), (1,)), ((), ())), preferred_element_type=F32
            )
            for i in range(chunk):
                lanes = pl.ds(pl.multiple_of((base + i) * wide, 128), wide)
                block = product[:, i * wide : (i + 1) * wide].reshape(rows_b, points, wide)
                plain = jnp.sum(fr_ref[:, lanes][None] * block, axis=1)
                turned = jnp.sum(fi_ref[:, lanes][None] * block, axis=1)
                result = (plain + swap_parts(turned)) * (1.0 / points)
                t_ref[group, base + i] = result.astype(BF16)
        return carry

    lax.fori_loop(0, chunks, backward, 0)


def body(
    amplitudes,
    valence_orbitals,
    conduction_orbitals,
    screened,
    coupling,
    grid_index,
    valence_index,
    conduction_index,
    valence_table,
    conduction_table,
):
    points = grid_index.shape[0]
    groups = lax.axis_size("grp")
    bands_c, nmu = conduction_orbitals.shape[2:]
    vectors = amplitudes.shape[3]
    wide = 2 * bands_c
    owned = screened.shape[2] // nmu
    split = groups if owned % groups == 0 else 1
    share = owned // split
    rows_b = share * vectors
    table_r, table_i = lattice_tables(grid_index)
    table_r = jnp.repeat(table_r, wide, axis=1)
    table_i = jnp.repeat(table_i, wide, axis=1)
    trials = amplitudes[0, 0]
    val = valence_orbitals[0]
    vr, vi = val[0], val[1]

    def first(x, y):
        return jnp.einsum("vm,jvc->mjc", x, y, preferred_element_type=F32)

    b_real = first(vr, trials[0]) - first(vi, trials[1])
    b_imag = first(vr, trials[1]) + first(vi, trials[0])
    b = jnp.concatenate([b_real, b_imag], axis=-1).astype(BF16)
    if split > 1:
        b = b.reshape(points * split, rows_b, wide)
        b = lax.all_to_all(b, ("ka", "grp"), split_axis=0, concat_axis=0, tiled=True)
        b = b.reshape(points, groups, rows_b, wide)
    else:
        b = b.reshape(points, rows_b, wide)
        b = lax.all_to_all(b, "ka", split_axis=0, concat_axis=0, tiled=True)
        b = lax.all_gather(b, "grp", axis=1)
    cond = jnp.concatenate([conduction_orbitals[0, 0], conduction_orbitals[0, 1]], axis=-1)
    cond = lax.all_gather(cond, "ka")
    chunk = 4
    rows = rows_b * points
    vmem = pl.BlockSpec(memory_space=pltpu.VMEM)
    hbm = pl.BlockSpec(memory_space=pl.ANY)
    t = pl.pallas_call(
        functools.partial(middle_kernel, split, chunk, rows_b),
        out_shape=jax.ShapeDtypeStruct((groups, points, rows_b, wide), BF16),
        in_specs=[vmem, vmem, vmem, vmem, hbm, hbm],
        out_specs=vmem,
        scratch_shapes=[
            pltpu.VMEM((rows, chunk * wide), BF16),
            pltpu.VMEM((chunk * wide, 2 * nmu), BF16),
            pltpu.VMEM((groups, rows, 2 * nmu), F32),
            pltpu.VMEM((groups, rows, 2 * nmu), BF16),
            pltpu.VMEM((2, points, share * nmu), F32),
            pltpu.VMEM((2, points, share * nmu), F32),
            pltpu.SemaphoreType.DMA((2,)),
        ],
        compiler_params=pltpu.CompilerParams(vmem_limit_bytes=60 * 2**20),
    )(table_r, table_i, b, cond, screened, coupling)
    if split > 1:
        t = t.swapaxes(0, 1).reshape(points * split, rows_b, wide)
        t = lax.all_to_all(t, ("ka", "grp"), split_axis=0, concat_axis=0, tiled=True)
    else:
        t = lax.dynamic_index_in_dim(t, lax.axis_index("grp"), 0, keepdims=False)
        t = lax.all_to_all(t, "ka", split_axis=0, concat_axis=0, tiled=True)
    t = t.reshape(nmu, vectors, wide)
    d_real = jnp.einsum("vm,mjc->jvc", vr, t, preferred_element_type=F32)
    d_imag = jnp.einsum("vm,mjc->jvc", vi, t, preferred_element_type=F32)
    kern_real = d_real[..., :bands_c] + d_imag[..., bands_c:]
    kern_imag = d_imag[..., :bands_c] - d_real[..., bands_c:]
    kernel = jnp.stack([kern_real, kern_imag])
    energy = (
        lookup(conduction_index, conduction_table)[0][None, :]
        - lookup(valence_index, valence_table)[0][:, None]
    )
    group_sign = 1.0 - 2.0 * lax.axis_index("grp").astype(F32)
    result = group_sign * (energy * trials.astype(F32) - kernel)
    return result.astype(BF16)[None, None]


def solution(mesh):
    placed = (
        P("grp", "ka", None, None, None, None),
        P("ka", None, None, None),
        P("ka", None, None, None),
        P(None, None, "ka"),
        P(None, None, "ka"),
        P(),
        P("ka", None),
        P("ka", None),
        P(),
        P(),
    )
    return jax.shard_map(
        body,
        mesh=mesh,
        in_specs=placed,
        out_specs=P("grp", "ka", None, None, None, None),
        check_vma=False,
    )
```

```python
import functools

import jax
import jax.numpy as jnp
from jax import lax
from jax.experimental import pallas as pl
from jax.experimental.pallas import tpu as pltpu
from jax.sharding import PartitionSpec as P

F32 = jnp.float32
BF16 = jnp.bfloat16


def lattice_tables(grid_index):
    points = grid_index.shape[0]
    grid_side = points // 4
    lattice = jnp.arange(points, dtype=jnp.int32)
    turn_count = lattice[:, None] // grid_side * (grid_index[None, :] // grid_side) * grid_side
    turn_count = turn_count + 4 * (lattice[:, None] % grid_side) * (grid_index[None, :] % grid_side)
    turn_count = turn_count % points
    phases = turn_count.astype(F32) * (2.0 * jnp.pi / points)
    return (jnp.cos(phases), -jnp.sin(phases))


MESH = pl.DeviceIdType.MESH
ROWS = 16


def swap_parts(values):
    half = values.shape[-1] // 2
    turned = pltpu.roll(values, half, values.ndim - 1)
    lanes = lax.broadcasted_iota(jnp.int32, values.shape, values.ndim - 1)
    return jnp.where(lanes < half, -turned, turned)


def diagonal(size):
    return lax.broadcasted_iota(jnp.int32, (size, size), 0) == lax.broadcasted_iota(
        jnp.int32, (size, size), 1
    )


def levels_of(index_row, table_row):
    size = index_row.shape[1]
    column = jnp.sum(jnp.where(diagonal(size), index_row.astype(F32), 0.0), axis=1, keepdims=True)
    steps = lax.broadcasted_iota(jnp.int32, (size, table_row.shape[1]), 1).astype(F32)
    return jnp.sum(jnp.where(steps == column, table_row, 0.0), axis=1, keepdims=True)


def whole_kernel(split, share, chunk, amp_ref, val_ref, cond_ref, table_ref, vidx_ref, cidx_ref, vtab_ref,
                 ctab_ref, screened_ref, coupling_ref, out_ref, fr, fi, gathered, b_send, b_recv, t_send,
                 t_recv, left, weight, spec, mixed, scr, cpl, load_sem, own_sem, c_send_sem, c_sem,
                 b_send_sem, b_sem, t_send_sem, t_sem):
    points = table_ref.shape[1]
    half_c, nmu = cond_ref.shape[2:]
    vectors = amp_ref.shape[3]
    wide = 2 * half_c
    width = scr.shape[2]
    rows = share * points
    devices = 2 * points
    slots = points * split
    grp, ka = lax.axis_index("grp"), lax.axis_index("ka")
    place = ka * split + (grp if split > 1 else 0)

    start = grp * width if split > 1 else 0
    span = pl.ds(pl.multiple_of(start, 128), width)
    load_s = pltpu.make_async_copy(screened_ref.at[:, :, span], scr, load_sem.at[0])
    load_c = pltpu.make_async_copy(coupling_ref.at[:, :, span], cpl, load_sem.at[1])
    load_s.start()
    load_c.start()
    own = pltpu.make_async_copy(cond_ref.at[0], gathered.at[ka], own_sem)
    own.start()

    barrier = pltpu.get_barrier_semaphore()

    def greet(i, carry):
        to = lax.rem(grp * points + ka + i, devices)
        pl.semaphore_signal(
            barrier, inc=1, device_id=(to // points, lax.rem(to, points)), device_id_type=MESH
        )
        return carry

    lax.fori_loop(1, devices, greet, 0)

    padded = slots * ROWS
    line = lax.broadcasted_iota(jnp.int32, (padded, nmu), 0)
    column = lax.broadcasted_iota(jnp.int32, (padded, nmu), 1)
    inner = line % ROWS
    spread = ((inner < share) & (column == line // ROWS * share + inner)).astype(BF16)
    nt = (((1,), (1,)), ((), ()))
    up_r = lax.dot_general(spread, val_ref[0, 0], nt, preferred_element_type=F32).astype(BF16)
    up_i = lax.dot_general(spread, val_ref[0, 1], nt, preferred_element_type=F32).astype(BF16)
    parts_r, parts_i = [], []
    for j in range(vectors):
        parts_r += [amp_ref[0, 0, 0, j], amp_ref[0, 0, 1, j]]
        parts_i += [-amp_ref[0, 0, 1, j], amp_ref[0, 0, 0, j]]
    b = jnp.dot(up_r, jnp.concatenate(parts_r, axis=1), preferred_element_type=F32)
    b = b + jnp.dot(up_i, jnp.concatenate(parts_i, axis=1), preferred_element_type=F32)
    b_send[...] = b.astype(BF16).reshape(b_send.shape)
    for k in range(points):
        fr[:, k * wide : (k + 1) * wide] = jnp.broadcast_to(table_ref[0, :, k : k + 1], (points, wide))
        fi[:, k * wide : (k + 1) * wide] = jnp.broadcast_to(table_ref[1, :, k : k + 1], (points, wide))

    own.wait()
    pl.semaphore_wait(barrier, devices - 1)

    high = points // 4
    hi, mi, lo = ka // 4, ka // 2 % 2, ka % 2
    far = 1 - grp

    def pass_on(k, part, to_grp, to_ka):
        pltpu.make_async_remote_copy(
            src_ref=gathered.at[k, part],
            dst_ref=gathered.at[k, part],
            send_sem=c_send_sem,
            recv_sem=c_sem.at[k, part],
            device_id=(to_grp, to_ka),
            device_id_type=MESH,
        ).start()

    def arrived(k, part):
        pltpu.make_async_copy(gathered.at[k, part], gathered.at[k, part], c_sem.at[k, part]).wait()

    to_mi = hi * 4 + (1 - mi) * 2 + lo
    to_lo = hi * 4 + mi * 2 + (1 - lo)

    def lane(step, middle, low):
        return lax.rem(hi + high - step, high) * 4 + middle * 2 + low

    def out_first(s, carry):
        pass_on(ka, grp, grp, lax.rem(hi + s, high) * 4 + mi * 2 + lo)
        return carry

    lax.fori_loop(1, high, out_first, 0)
    pass_on(ka, grp, grp, to_mi)
    pass_on(ka, grp, grp, to_lo)
    pass_on(ka, far, grp, to_lo)

    def send_b(i, carry):
        to = lax.rem(grp * points + ka + i, devices)
        to_grp, to_ka = to // points, lax.rem(to, points)
        slot = to_ka * split + (to_grp if split > 1 else 0)
        pltpu.make_async_remote_copy(
            src_ref=b_send.at[slot],
            dst_ref=b_recv.at[ka * 2 + grp],
            send_sem=b_send_sem,
            recv_sem=b_sem,
            device_id=(to_grp, to_ka),
            device_id_type=MESH,
        ).start()
        return carry

    lax.fori_loop(1, devices, send_b, 0)
    pltpu.make_async_copy(b_send.at[place], b_recv.at[ka * 2 + grp], b_sem).start()

    def second(s, carry):
        k = lane(s, mi, lo)
        arrived(k, grp)
        pass_on(k, grp, grp, to_mi)
        pass_on(k, grp, far, ka)
        pass_on(k, grp, grp, to_lo)
        return carry

    def third(s, carry):
        k = lane(s, 1 - mi, lo)
        arrived(k, grp)
        pass_on(k, grp, far, ka)
        pass_on(k, grp, grp, to_lo)
        return carry

    def fourth(s, carry):
        k = lane(s, mi, lo)
        arrived(k, far)
        pass_on(k, far, grp, to_lo)
        return carry

    def fifth(s, carry):
        k = lane(s, 1 - mi, lo)
        arrived(k, far)
        pass_on(k, far, grp, to_lo)
        return carry

    def last(s, carry):
        for middle in range(2):
            k = lane(s, middle, 1 - lo)
            arrived(k, 0)
            arrived(k, 1)
        return carry

    lax.fori_loop(1, high, second, 0)
    lax.fori_loop(0, high, third, 0)
    lax.fori_loop(1, high, fourth, 0)
    lax.fori_loop(0, high, fifth, 0)
    lax.fori_loop(0, high, last, 0)
    pltpu.make_async_copy(b_recv, b_recv, b_sem).wait()

    chunks = points // chunk

    def fill(base):
        for i in range(chunk):
            real, imag = gathered[base + i, 0], gathered[base + i, 1]
            top = pl.ds(i * wide, half_c)
            bottom = pl.ds(i * wide + half_c, half_c)
            weight[top, :nmu] = real
            weight[top, nmu:] = imag
            weight[bottom, :nmu] = -imag
            weight[bottom, nmu:] = real

    def forward(step, carry):
        base = step * chunk
        fill(base)
        for group in range(2):
            for i in range(chunk):
                lanes = pl.ds(pl.multiple_of((base + i) * wide, 128), wide)
                table_r = fr[:, lanes]
                table_i = fi[:, lanes]
                for j in range(vectors):
                    data = b_recv[(base + i) * 2 + group, :, j * wide : (j + 1) * wide].astype(F32)[:share]
                    turned = swap_parts(data)
                    block = table_r[None] * data[:, None, :] + table_i[None] * turned[:, None, :]
                    left[j * rows : (j + 1) * rows, i * wide : (i + 1) * wide] = block.reshape(
                        rows, wide
                    ).astype(BF16)
            part = jnp.dot(left[...], weight[...], preferred_element_type=F32)

            @pl.when(step == 0)
            def _():
                spec[group] = part

            @pl.when(step > 0)
            def _():
                spec[group] += part

        return carry

    lax.fori_loop(0, chunks, forward, 0)
    load_s.wait()
    load_c.wait()

    def weigh(mu, carry):
        lanes = pl.ds(pl.multiple_of(mu * nmu, 128), nmu)
        sr, si = scr[0, :, lanes], scr[1, :, lanes]
        cr, ci = cpl[0, :, lanes], cpl[1, :, lanes]
        for j in range(vectors):
            at = pl.ds(pl.multiple_of(j * rows + mu * points, ROWS), points)
            fields = [(spec[g, at, :nmu], spec[g, at, nmu:]) for g in range(2)]
            for g in range(2):
                (ar, ai), (br, bi) = fields[g], fields[1 - g]
                real = sr * ar - si * ai + cr * br - ci * bi
                imag = sr * ai + si * ar + cr * bi + ci * br
                mixed[g, at, :nmu] = real.astype(BF16)
                mixed[g, at, nmu:] = (-imag).astype(BF16)
        return carry

    lax.fori_loop(0, share, weigh, 0)

    def backward(step, carry):
        base = lax.rem(step + hi, chunks) * chunk
        fill(base)
        for group in range(2):
            product = lax.dot_general(mixed[group], weight[...], nt, preferred_element_type=F32)
            for i in range(chunk):
                lanes = pl.ds(pl.multiple_of((base + i) * wide, 128), wide)
                slot = (base + i) * 2 + group
                for j in range(vectors):
                    block = product[j * rows : (j + 1) * rows, i * wide : (i + 1) * wide]
                    block = block.reshape(share, points, wide)
                    plain = jnp.sum(fr[:, lanes][None] * block, axis=1)
                    turned = jnp.sum(fi[:, lanes][None] * block, axis=1)
                    result = (plain + swap_parts(turned)) * (1.0 / points)
                    result = jnp.concatenate([result, jnp.zeros((ROWS - share, wide), F32)], axis=0)
                    t_send[slot, :, j * wide : (j + 1) * wide] = result.astype(BF16)
        for group in range(2):
            for i in range(chunk):
                k = base + i
                here = (k == ka) & (group == grp)
                wanted = (group == grp) if split == 1 else (k >= 0)

                @pl.when(here)
                def _():
                    pltpu.make_async_copy(t_send.at[k * 2 + group], t_recv.at[place], t_sem).start()

                @pl.when(jnp.logical_not(here) & wanted)
                def _():
                    pltpu.make_async_remote_copy(
                        src_ref=t_send.at[k * 2 + group],
                        dst_ref=t_recv.at[place],
                        send_sem=t_send_sem,
                        recv_sem=t_sem,
                        device_id=(group, k),
                        device_id_type=MESH,
                    ).start()

        return carry

    lax.fori_loop(0, chunks, backward, 0)

    energy_v = levels_of(vidx_ref[...], vtab_ref[...])
    energy_c = levels_of(cidx_ref[...], ctab_ref[...])
    energy_c = jnp.sum(jnp.where(diagonal(half_c), energy_c, 0.0), axis=0, keepdims=True)
    energy = energy_c - energy_v
    line = lax.broadcasted_iota(jnp.int32, (nmu, padded), 0)
    column = lax.broadcasted_iota(jnp.int32, (nmu, padded), 1)
    inner = column % ROWS
    spread = ((inner < share) & (line == column // ROWS * share + inner)).astype(BF16)
    down_r = jnp.dot(val_ref[0, 0], spread, preferred_element_type=F32).astype(BF16)
    down_i = jnp.dot(val_ref[0, 1], spread, preferred_element_type=F32).astype(BF16)
    group_sign = 1.0 - 2.0 * grp.astype(F32)

    pltpu.make_async_copy(t_recv, t_recv, t_sem).wait()
    blocks = t_recv[...].reshape(padded, vectors * wide)
    d_real = jnp.dot(down_r, blocks, preferred_element_type=F32)
    d_imag = jnp.dot(down_i, blocks, preferred_element_type=F32)
    for j in range(vectors):
        at, mid, end = j * wide, j * wide + half_c, (j + 1) * wide
        kern_real = d_real[:, at:mid] + d_imag[:, mid:end]
        kern_imag = d_imag[:, at:mid] - d_real[:, mid:end]
        for part, kern in enumerate((kern_real, kern_imag)):
            trial = amp_ref[0, 0, part, j].astype(F32)
            out_ref[0, 0, part, j] = (group_sign * (energy * trial - kern)).astype(BF16)

    sent = pl.ds(0, points - 1)
    pltpu.make_async_copy(gathered.at[sent], gathered.at[sent], c_send_sem).wait()
    sent = pl.ds(0, devices - 1)
    pltpu.make_async_copy(b_recv.at[sent], b_recv.at[sent], b_send_sem).wait()
    sent = pl.ds(0, slots - 1)
    pltpu.make_async_copy(t_recv.at[sent], t_recv.at[sent], t_send_sem).wait()


def body(
    amplitudes,
    valence_orbitals,
    conduction_orbitals,
    screened,
    coupling,
    grid_index,
    valence_index,
    conduction_index,
    valence_table,
    conduction_table,
):
    points = grid_index.shape[0]
    groups = lax.axis_size("grp")
    bands_c, nmu = conduction_orbitals.shape[2:]
    vectors = amplitudes.shape[3]
    wide = 2 * bands_c
    owned = screened.shape[2] // nmu
    split = groups if owned % groups == 0 else 1
    share = owned // split
    table = jnp.stack(lattice_tables(grid_index))
    chunk = 4
    rows = share * points * vectors
    block = (ROWS, vectors * wide)
    vmem = pl.BlockSpec(memory_space=pltpu.VMEM)
    hbm = pl.BlockSpec(memory_space=pl.ANY)
    return pl.pallas_call(
        functools.partial(whole_kernel, split, share, chunk),
        out_shape=jax.ShapeDtypeStruct(amplitudes.shape, BF16),
        in_specs=[vmem] * 8 + [hbm] * 2,
        out_specs=vmem,
        scratch_shapes=[
            pltpu.VMEM((points, points * wide), F32),
            pltpu.VMEM((points, points * wide), F32),
            pltpu.VMEM((points, 2, bands_c, nmu), BF16),
            pltpu.VMEM((points * split,) + block, BF16),
            pltpu.VMEM((points * groups,) + block, BF16),
            pltpu.VMEM((points * groups,) + block, BF16),
            pltpu.VMEM((points * split,) + block, BF16),
            pltpu.VMEM((rows, chunk * wide), BF16),
            pltpu.VMEM((chunk * wide, 2 * nmu), BF16),
            pltpu.VMEM((groups, rows, 2 * nmu), F32),
            pltpu.VMEM((groups, rows, 2 * nmu), BF16),
            pltpu.VMEM((2, points, share * nmu), F32),
            pltpu.VMEM((2, points, share * nmu), F32),
            pltpu.SemaphoreType.DMA((2,)),
            pltpu.SemaphoreType.DMA,
            pltpu.SemaphoreType.DMA,
            pltpu.SemaphoreType.DMA((points, 2)),
            pltpu.SemaphoreType.DMA,
            pltpu.SemaphoreType.DMA,
            pltpu.SemaphoreType.DMA,
            pltpu.SemaphoreType.DMA,
        ],
        compiler_params=pltpu.CompilerParams(
            collective_id=0, has_side_effects=True, vmem_limit_bytes=60 * 2**20
        ),
    )(
        amplitudes,
        valence_orbitals,
        conduction_orbitals,
        table,
        valence_index,
        conduction_index,
        valence_table[None],
        conduction_table[None],
        screened,
        coupling,
    )


def solution(mesh):
    placed = (
        P("grp", "ka", None, None, None, None),
        P("ka", None, None, None),
        P("ka", None, None, None),
        P(None, None, "ka"),
        P(None, None, "ka"),
        P(),
        P("ka", None),
        P("ka", None),
        P(),
        P(),
    )
    return jax.shard_map(
        body,
        mesh=mesh,
        in_specs=placed,
        out_specs=P("grp", "ka", None, None, None, None),
        check_vma=False,
    )
```

```python
import functools

import jax
import jax.numpy as jnp
from jax import lax
from jax.experimental import pallas as pl
from jax.experimental.pallas import tpu as pltpu
from jax.sharding import PartitionSpec as P

F32 = jnp.float32
BF16 = jnp.bfloat16


def lattice_tables(grid_row):
    points = grid_row.shape[1]
    grid_side = points // 4
    lattice = lax.broadcasted_iota(jnp.int32, (points, points), 0)
    grid = jnp.broadcast_to(grid_row, (points, points))
    turn_count = lattice // grid_side * (grid // grid_side) * grid_side
    turn_count = turn_count + 4 * (lattice % grid_side) * (grid % grid_side)
    turn_count = turn_count % points
    phases = turn_count.astype(F32) * (2.0 * jnp.pi / points)
    return (jnp.cos(phases), -jnp.sin(phases))


MESH = pl.DeviceIdType.MESH
TILE = 8


def swap_parts(values):
    half = values.shape[-1] // 2
    turned = pltpu.roll(values, half, values.ndim - 1)
    lanes = lax.broadcasted_iota(jnp.int32, values.shape, values.ndim - 1)
    return jnp.where(lanes < half, -turned, turned)


def diagonal(size):
    return lax.broadcasted_iota(jnp.int32, (size, size), 0) == lax.broadcasted_iota(
        jnp.int32, (size, size), 1
    )


def levels_of(index_row, table_row):
    size = index_row.shape[1]
    column = jnp.sum(jnp.where(diagonal(size), index_row.astype(F32), 0.0), axis=1, keepdims=True)
    steps = lax.broadcasted_iota(jnp.int32, (size, table_row.shape[1]), 1).astype(F32)
    return jnp.sum(jnp.where(steps == column, table_row, 0.0), axis=1, keepdims=True)


def whole_kernel(split, share, chunk, amp_ref, val_ref, cond_ref, grid_ref, vidx_ref, cidx_ref, vtab_ref,
                 ctab_ref, screened_ref, coupling_ref, out_ref, fr, fi, gathered, b_send, b_recv, t_send,
                 t_recv, left, weight, spec, mixed, scr, cpl, load_sem, own_sem, c_send_sem, c_sem,
                 b_send_sem, b_sem, t_send_sem, t_sem):
    points = grid_ref.shape[1]
    half_c, nmu = cond_ref.shape[2:]
    vectors = amp_ref.shape[3]
    wide = 2 * half_c
    width = scr.shape[2]
    rows = share * points
    devices = 2 * points
    slots = points * split
    used = share * vectors
    tall = b_send.shape[1] * TILE
    grp, ka = lax.axis_index("grp"), lax.axis_index("ka")
    place = ka * split + (grp if split > 1 else 0)

    start = grp * width if split > 1 else 0
    span = pl.ds(pl.multiple_of(start, 128), width)
    load_s = pltpu.make_async_copy(screened_ref.at[:, :, span], scr, load_sem.at[0])
    load_c = pltpu.make_async_copy(coupling_ref.at[:, :, span], cpl, load_sem.at[1])
    load_s.start()
    load_c.start()
    own = pltpu.make_async_copy(cond_ref.at[0], gathered.at[ka], own_sem)
    own.start()

    barrier = pltpu.get_barrier_semaphore()

    def greet(i, carry):
        to = lax.rem(grp * points + ka + i, devices)
        pl.semaphore_signal(
            barrier, inc=1, device_id=(to // points, lax.rem(to, points)), device_id_type=MESH
        )
        return carry

    lax.fori_loop(1, devices, greet, 0)

    padded = slots * tall
    line = lax.broadcasted_iota(jnp.int32, (padded, nmu), 0)
    column = lax.broadcasted_iota(jnp.int32, (padded, nmu), 1)
    inner = line % tall
    spread = (inner < used) & (column == line // tall * share + inner % share)
    spread = spread.astype(F32).astype(BF16)
    nt = (((1,), (1,)), ((), ()))
    up_r = lax.dot_general(spread, val_ref[0, 0], nt, preferred_element_type=F32).astype(BF16)
    up_i = lax.dot_general(spread, val_ref[0, 1], nt, preferred_element_type=F32).astype(BF16)
    which = lax.broadcasted_iota(jnp.int32, (padded, wide), 0) % tall // share
    b = jnp.zeros((padded, wide), F32)
    for j in range(vectors):
        real, imag = amp_ref[0, 0, 0, j], amp_ref[0, 0, 1, j]
        term = jnp.dot(up_r, jnp.concatenate([real, imag], axis=1), preferred_element_type=F32)
        term = term + jnp.dot(up_i, jnp.concatenate([-imag, real], axis=1), preferred_element_type=F32)
        b = jnp.where(which == j, term, b)
    b_send[...] = b.reshape(b_send.shape).astype(BF16)
    table_r, table_i = lattice_tables(grid_ref[...])
    for k in range(points):
        fr[:, k * wide : (k + 1) * wide] = jnp.broadcast_to(table_r[:, k : k + 1], (points, wide))
        fi[:, k * wide : (k + 1) * wide] = jnp.broadcast_to(table_i[:, k : k + 1], (points, wide))

    own.wait()
    pl.semaphore_wait(barrier, devices - 1)

    high = points // 4
    hi, mi, lo = ka // 4, ka // 2 % 2, ka % 2
    far = 1 - grp

    def pass_on(k, part, to_grp, to_ka):
        pltpu.make_async_remote_copy(
            src_ref=gathered.at[k, part],
            dst_ref=gathered.at[k, part],
            send_sem=c_send_sem,
            recv_sem=c_sem.at[k, part],
            device_id=(to_grp, to_ka),
            device_id_type=MESH,
        ).start()

    def arrived(k, part):
        pltpu.make_async_copy(gathered.at[k, part], gathered.at[k, part], c_sem.at[k, part]).wait()

    to_mi = hi * 4 + (1 - mi) * 2 + lo
    to_lo = hi * 4 + mi * 2 + (1 - lo)

    def lane(step, middle, low):
        return lax.rem(hi + high - step, high) * 4 + middle * 2 + low

    def out_first(s, carry):
        pass_on(ka, grp, grp, lax.rem(hi + s, high) * 4 + mi * 2 + lo)
        return carry

    lax.fori_loop(1, high, out_first, 0)
    pass_on(ka, grp, grp, to_mi)
    pass_on(ka, grp, grp, to_lo)
    pass_on(ka, far, grp, to_lo)

    def send_b(i, carry):
        to = lax.rem(grp * points + ka + i, devices)
        to_grp, to_ka = to // points, lax.rem(to, points)
        slot = to_ka * split + (to_grp if split > 1 else 0)
        pltpu.make_async_remote_copy(
            src_ref=b_send.at[slot],
            dst_ref=b_recv.at[ka * 2 + grp],
            send_sem=b_send_sem,
            recv_sem=b_sem,
            device_id=(to_grp, to_ka),
            device_id_type=MESH,
        ).start()
        return carry

    lax.fori_loop(1, devices, send_b, 0)
    pltpu.make_async_copy(b_send.at[place], b_recv.at[ka * 2 + grp], b_sem).start()

    def second(s, carry):
        k = lane(s, mi, lo)
        arrived(k, grp)
        pass_on(k, grp, grp, to_mi)
        pass_on(k, grp, far, ka)
        pass_on(k, grp, grp, to_lo)
        return carry

    def third(s, carry):
        k = lane(s, 1 - mi, lo)
        arrived(k, grp)
        pass_on(k, grp, far, ka)
        pass_on(k, grp, grp, to_lo)
        return carry

    def fourth(s, carry):
        k = lane(s, mi, lo)
        arrived(k, far)
        pass_on(k, far, grp, to_lo)
        return carry

    def fifth(s, carry):
        k = lane(s, 1 - mi, lo)
        arrived(k, far)
        pass_on(k, far, grp, to_lo)
        return carry

    def last(s, carry):
        for middle in range(2):
            k = lane(s, middle, 1 - lo)
            arrived(k, 0)
            arrived(k, 1)
        return carry

    def relay(s):
        second(s, 0)
        third(s, 0)
        fourth(s, 0)
        fifth(s, 0)

    chunks = points // chunk

    def fill(base):
        for i in range(chunk):
            real, imag = gathered[base + i, 0], gathered[base + i, 1]
            top = pl.ds(i * wide, half_c)
            bottom = pl.ds(i * wide + half_c, half_c)
            weight[top, :nmu] = real
            weight[top, nmu:] = imag
            weight[bottom, :nmu] = -imag
            weight[bottom, nmu:] = real

    def forward(step):
        base = lax.rem(hi + high - step, high) * chunk
        fill(base)
        for group in range(2):
            for i in range(chunk):
                lanes = pl.ds(pl.multiple_of((base + i) * wide, 128), wide)
                data = b_recv[(base + i) * 2 + group].astype(F32).reshape(tall, wide)[:used]
                turned = swap_parts(data)
                block = fr[:, lanes][None] * data[:, None, :] + fi[:, lanes][None] * turned[:, None, :]
                left[:, i * wide : (i + 1) * wide] = block.reshape(used * points, wide).astype(BF16)
            part = jnp.dot(left[...], weight[...], preferred_element_type=F32)

            @pl.when(step == 0)
            def _():
                spec[group] = part

            @pl.when(step > 0)
            def _():
                spec[group] += part

    third(0, 0)
    fifth(0, 0)

    def relay_and_use(s, carry):
        relay(s)

        @pl.when(s == 1)
        def _():
            pltpu.make_async_copy(b_recv, b_recv, b_sem).wait()

        last(s - 1, 0)
        forward(s - 1)
        return carry

    lax.fori_loop(1, high, relay_and_use, 0)
    last(high - 1, 0)
    forward(high - 1)
    load_s.wait()
    load_c.wait()

    def weigh(mu, carry):
        lanes = pl.ds(pl.multiple_of(mu * nmu, 128), nmu)
        sr, si = scr[0, :, lanes], scr[1, :, lanes]
        cr, ci = cpl[0, :, lanes], cpl[1, :, lanes]
        for j in range(vectors):
            at = pl.ds(pl.multiple_of(j * rows + mu * points, 16), points)
            fields = [(spec[g, at, :nmu], spec[g, at, nmu:]) for g in range(2)]
            for g in range(2):
                (ar, ai), (br, bi) = fields[g], fields[1 - g]
                real = sr * ar - si * ai + cr * br - ci * bi
                imag = sr * ai + si * ar + cr * bi + ci * br
                mixed[g, at, :nmu] = real.astype(BF16)
                mixed[g, at, nmu:] = (-imag).astype(BF16)
        return carry

    lax.fori_loop(0, share, weigh, 0)

    def backward(step, carry):
        base = lax.rem(step + 1 + hi, chunks) * chunk
        fill(base)
        for group in range(2):
            product = lax.dot_general(mixed[group], weight[...], nt, preferred_element_type=F32)
            for i in range(chunk):
                lanes = pl.ds(pl.multiple_of((base + i) * wide, 128), wide)
                block = product[:, i * wide : (i + 1) * wide].reshape(used, points, wide)
                plain = jnp.sum(fr[:, lanes][None] * block, axis=1)
                turned = jnp.sum(fi[:, lanes][None] * block, axis=1)
                result = (plain + swap_parts(turned)) * (1.0 / points)
                if used < tall:
                    result = jnp.concatenate([result, jnp.zeros((tall - used, wide), F32)], axis=0)
                t_send[(base + i) * 2 + group] = result.reshape(t_send.shape[1:]).astype(BF16)
        for group in range(2):
            for i in range(chunk):
                k = base + i
                here = (k == ka) & (group == grp)
                wanted = (group == grp) if split == 1 else (k >= 0)

                @pl.when(here)
                def _():
                    pltpu.make_async_copy(t_send.at[k * 2 + group], t_recv.at[place], t_sem).start()

                @pl.when(jnp.logical_not(here) & wanted)
                def _():
                    pltpu.make_async_remote_copy(
                        src_ref=t_send.at[k * 2 + group],
                        dst_ref=t_recv.at[place],
                        send_sem=t_send_sem,
                        recv_sem=t_sem,
                        device_id=(group, k),
                        device_id_type=MESH,
                    ).start()

        return carry

    lax.fori_loop(0, chunks, backward, 0)

    energy_v = levels_of(vidx_ref[...], vtab_ref[...])
    energy_c = levels_of(cidx_ref[...], ctab_ref[...])
    energy_c = jnp.sum(jnp.where(diagonal(half_c), energy_c, 0.0), axis=0, keepdims=True)
    energy = energy_c - energy_v
    line = lax.broadcasted_iota(jnp.int32, (nmu, padded), 0)
    column = lax.broadcasted_iota(jnp.int32, (nmu, padded), 1)
    inner = column % tall
    spread = (inner < used) & (line == column // tall * share + inner % share)
    spread = spread.astype(F32).astype(BF16)
    down_r = jnp.dot(val_ref[0, 0], spread, preferred_element_type=F32)
    down_i = jnp.dot(val_ref[0, 1], spread, preferred_element_type=F32)
    which = lax.broadcasted_iota(jnp.int32, (half_c, padded), 1) % tall // share
    group_sign = 1.0 - 2.0 * grp.astype(F32)

    pltpu.make_async_copy(t_recv, t_recv, t_sem).wait()
    blocks = t_recv[...].astype(F32).reshape(padded, wide).astype(BF16)
    for j in range(vectors):
        mine_r = jnp.where(which == j, down_r, 0.0).astype(BF16)
        mine_i = jnp.where(which == j, down_i, 0.0).astype(BF16)
        d_real = jnp.dot(mine_r, blocks, preferred_element_type=F32)
        d_imag = jnp.dot(mine_i, blocks, preferred_element_type=F32)
        kern_real = d_real[:, :half_c] + d_imag[:, half_c:]
        kern_imag = d_imag[:, :half_c] - d_real[:, half_c:]
        for part, kern in enumerate((kern_real, kern_imag)):
            trial = amp_ref[0, 0, part, j].astype(F32)
            out_ref[0, 0, part, j] = (group_sign * (energy * trial - kern)).astype(BF16)

    sent = pl.ds(0, points - 1)
    pltpu.make_async_copy(gathered.at[sent], gathered.at[sent], c_send_sem).wait()
    sent = pl.ds(0, devices - 1)
    pltpu.make_async_copy(b_recv.at[sent], b_recv.at[sent], b_send_sem).wait()
    sent = pl.ds(0, slots - 1)
    pltpu.make_async_copy(t_recv.at[sent], t_recv.at[sent], t_send_sem).wait()


def body(
    amplitudes,
    valence_orbitals,
    conduction_orbitals,
    screened,
    coupling,
    grid_index,
    valence_index,
    conduction_index,
    valence_table,
    conduction_table,
):
    points = grid_index.shape[0]
    groups = lax.axis_size("grp")
    bands_c, nmu = conduction_orbitals.shape[2:]
    vectors = amplitudes.shape[3]
    wide = 2 * bands_c
    owned = screened.shape[2] // nmu
    split = groups if owned % groups == 0 else 1
    share = owned // split
    chunk = 4
    rows = share * points * vectors
    block = (-(-share * vectors // TILE), TILE, wide)
    vmem = pl.BlockSpec(memory_space=pltpu.VMEM)
    hbm = pl.BlockSpec(memory_space=pl.ANY)
    return pl.pallas_call(
        functools.partial(whole_kernel, split, share, chunk),
        out_shape=jax.ShapeDtypeStruct(amplitudes.shape, BF16),
        in_specs=[vmem] * 8 + [hbm] * 2,
        out_specs=vmem,
        scratch_shapes=[
            pltpu.VMEM((points, points * wide), F32),
            pltpu.VMEM((points, points * wide), F32),
            pltpu.VMEM((points, 2, bands_c, nmu), BF16),
            pltpu.VMEM((points * split,) + block, BF16),
            pltpu.VMEM((points * groups,) + block, BF16),
            pltpu.VMEM((points * groups,) + block, BF16),
            pltpu.VMEM((points * split,) + block, BF16),
            pltpu.VMEM((rows, chunk * wide), BF16),
            pltpu.VMEM((chunk * wide, 2 * nmu), BF16),
            pltpu.VMEM((groups, rows, 2 * nmu), F32),
            pltpu.VMEM((groups, rows, 2 * nmu), BF16),
            pltpu.VMEM((2, points, share * nmu), F32),
            pltpu.VMEM((2, points, share * nmu), F32),
            pltpu.SemaphoreType.DMA((2,)),
            pltpu.SemaphoreType.DMA,
            pltpu.SemaphoreType.DMA,
            pltpu.SemaphoreType.DMA((points, 2)),
            pltpu.SemaphoreType.DMA,
            pltpu.SemaphoreType.DMA,
            pltpu.SemaphoreType.DMA,
            pltpu.SemaphoreType.DMA,
        ],
        compiler_params=pltpu.CompilerParams(
            collective_id=0, has_side_effects=True, vmem_limit_bytes=60 * 2**20
        ),
    )(
        amplitudes,
        valence_orbitals,
        conduction_orbitals,
        grid_index[None],
        valence_index,
        conduction_index,
        valence_table[None],
        conduction_table[None],
        screened,
        coupling,
    )


def solution(mesh):
    placed = (
        P("grp", "ka", None, None, None, None),
        P("ka", None, None, None),
        P("ka", None, None, None),
        P(None, None, "ka"),
        P(None, None, "ka"),
        P(),
        P("ka", None),
        P("ka", None),
        P(),
        P(),
    )
    return jax.shard_map(
        body,
        mesh=mesh,
        in_specs=placed,
        out_specs=P("grp", "ka", None, None, None, None),
        check_vma=False,
    )
```

```python
import functools

import jax
import jax.numpy as jnp
from jax import lax
from jax.experimental import pallas as pl
from jax.experimental.pallas import tpu as pltpu
from jax.sharding import PartitionSpec as P

F32 = jnp.float32
BF16 = jnp.bfloat16


def lattice_tables(grid_row):
    points = grid_row.shape[1]
    grid_side = points // 4
    lattice = lax.broadcasted_iota(jnp.int32, (points, points), 0)
    grid = jnp.broadcast_to(grid_row, (points, points))
    turn_count = lattice // grid_side * (grid // grid_side) * grid_side
    turn_count = turn_count + 4 * (lattice % grid_side) * (grid % grid_side)
    turn_count = turn_count % points
    phases = turn_count.astype(F32) * (2.0 * jnp.pi / points)
    return (jnp.cos(phases), -jnp.sin(phases))


MESH = pl.DeviceIdType.MESH
TILE = 8


def swap_parts(values):
    half = values.shape[-1] // 2
    turned = pltpu.roll(values, half, values.ndim - 1)
    lanes = lax.broadcasted_iota(jnp.int32, values.shape, values.ndim - 1)
    return jnp.where(lanes < half, -turned, turned)


def diagonal(size):
    return lax.broadcasted_iota(jnp.int32, (size, size), 0) == lax.broadcasted_iota(
        jnp.int32, (size, size), 1
    )


def levels_of(index_row, table_row):
    size = index_row.shape[1]
    column = jnp.sum(jnp.where(diagonal(size), index_row.astype(F32), 0.0), axis=1, keepdims=True)
    steps = lax.broadcasted_iota(jnp.int32, (size, table_row.shape[1]), 1).astype(F32)
    return jnp.sum(jnp.where(steps == column, table_row, 0.0), axis=1, keepdims=True)


def whole_kernel(split, share, chunk, amp_ref, val_ref, cond_ref, grid_ref, vidx_ref, cidx_ref, vtab_ref,
                 ctab_ref, screened_ref, coupling_ref, out_ref, fr, fi, gathered, b_send, b_recv, t_send,
                 t_recv, left, weight, spec, mixed, scr, cpl, up, load_sem, own_sem, c_send_sem, c_sem,
                 b_send_sem, b_sem, t_send_sem, t_sem):
    points = grid_ref.shape[1]
    half_c, nmu = cond_ref.shape[2:]
    vectors = amp_ref.shape[3]
    wide = 2 * half_c
    width = scr.shape[2]
    rows = share * points
    devices = 2 * points
    slots = points * split
    used = share * vectors
    tall = b_send.shape[1] * TILE
    grp, ka = lax.axis_index("grp"), lax.axis_index("ka")
    place = ka * split + (grp if split > 1 else 0)

    start = grp * width if split > 1 else 0
    span = pl.ds(pl.multiple_of(start, 128), width)
    load_s = pltpu.make_async_copy(screened_ref.at[:, :, span], scr, load_sem.at[0])
    load_c = pltpu.make_async_copy(coupling_ref.at[:, :, span], cpl, load_sem.at[1])
    load_s.start()
    load_c.start()
    own = pltpu.make_async_copy(cond_ref.at[0], gathered.at[ka], own_sem)
    own.start()

    barrier = pltpu.get_barrier_semaphore()

    def greet(i, carry):
        to = lax.rem(grp * points + ka + i, devices)
        pl.semaphore_signal(
            barrier, inc=1, device_id=(to // points, lax.rem(to, points)), device_id_type=MESH
        )
        return carry

    lax.fori_loop(1, devices, greet, 0)

    padded = slots * tall
    position = lax.broadcasted_iota(jnp.int32, (1, padded), 1)
    inner = position % tall
    vector = inner // share
    target = jnp.where(inner < used, position // tall * share + inner % share, -1)
    spread = lax.broadcasted_iota(jnp.int32, (nmu, padded), 0) == target
    spread = spread.astype(F32).astype(BF16)
    nt = (((1,), (1,)), ((), ()))
    tn = (((0,), (0,)), ((), ()))
    trial_rows = []
    for part in range(2):
        plain = jnp.dot(val_ref[0, part], spread, preferred_element_type=F32)
        for j in range(vectors):
            at = (j * 2 + part) * half_c
            up[at : at + half_c] = jnp.where(vector == j, plain, 0.0).astype(BF16)
    for j in range(vectors):
        real, imag = amp_ref[0, 0, 0, j], amp_ref[0, 0, 1, j]
        trial_rows.append(jnp.concatenate([real, imag], axis=1))
        trial_rows.append(jnp.concatenate([-imag, real], axis=1))
    b = lax.dot_general(up[...], jnp.concatenate(trial_rows, axis=0), tn, preferred_element_type=F32)
    b_send[...] = b.reshape(b_send.shape).astype(BF16)
    table_r, table_i = lattice_tables(grid_ref[...])
    for k in range(points):
        fr[:, k * wide : (k + 1) * wide] = jnp.broadcast_to(table_r[:, k : k + 1], (points, wide))
        fi[:, k * wide : (k + 1) * wide] = jnp.broadcast_to(table_i[:, k : k + 1], (points, wide))

    own.wait()
    pl.semaphore_wait(barrier, devices - 1)

    high = points // 4
    hi, mi, lo = ka // 4, ka // 2 % 2, ka % 2
    far = 1 - grp

    def pass_on(k, part, to_grp, to_ka):
        pltpu.make_async_remote_copy(
            src_ref=gathered.at[k, part],
            dst_ref=gathered.at[k, part],
            send_sem=c_send_sem,
            recv_sem=c_sem.at[k, part],
            device_id=(to_grp, to_ka),
            device_id_type=MESH,
        ).start()

    def arrived(k, part):
        pltpu.make_async_copy(gathered.at[k, part], gathered.at[k, part], c_sem.at[k, part]).wait()

    to_mi = hi * 4 + (1 - mi) * 2 + lo
    to_lo = hi * 4 + mi * 2 + (1 - lo)

    def lane(step, middle, low):
        return lax.rem(hi + high - step, high) * 4 + middle * 2 + low

    def out_first(s, carry):
        pass_on(ka, grp, grp, lax.rem(hi + s, high) * 4 + mi * 2 + lo)
        return carry

    lax.fori_loop(1, high, out_first, 0)
    pass_on(ka, grp, grp, to_mi)
    pass_on(ka, grp, grp, to_lo)
    pass_on(ka, far, grp, to_lo)

    def send_b(i, carry):
        to = lax.rem(grp * points + ka + i, devices)
        to_grp, to_ka = to // points, lax.rem(to, points)
        slot = to_ka * split + (to_grp if split > 1 else 0)
        pltpu.make_async_remote_copy(
            src_ref=b_send.at[slot],
            dst_ref=b_recv.at[ka * 2 + grp],
            send_sem=b_send_sem,
            recv_sem=b_sem,
            device_id=(to_grp, to_ka),
            device_id_type=MESH,
        ).start()
        return carry

    lax.fori_loop(1, devices, send_b, 0)
    pltpu.make_async_copy(b_send.at[place], b_recv.at[ka * 2 + grp], b_sem).start()

    def second(s, carry):
        k = lane(s, mi, lo)
        arrived(k, grp)
        pass_on(k, grp, grp, to_mi)
        pass_on(k, grp, far, ka)
        pass_on(k, grp, grp, to_lo)
        return carry

    def third(s, carry):
        k = lane(s, 1 - mi, lo)
        arrived(k, grp)
        pass_on(k, grp, far, ka)
        pass_on(k, grp, grp, to_lo)
        return carry

    def fourth(s, carry):
        k = lane(s, mi, lo)
        arrived(k, far)
        pass_on(k, far, grp, to_lo)
        return carry

    def fifth(s, carry):
        k = lane(s, 1 - mi, lo)
        arrived(k, far)
        pass_on(k, far, grp, to_lo)
        return carry

    def last(s, carry):
        for middle in range(2):
            k = lane(s, middle, 1 - lo)
            arrived(k, 0)
            arrived(k, 1)
        return carry

    lax.fori_loop(1, high, second, 0)
    lax.fori_loop(0, high, third, 0)
    fifth(0, 0)
    pltpu.make_async_copy(b_recv, b_recv, b_sem).wait()

    chunks = points // chunk

    def fill(base):
        for i in range(chunk):
            real, imag = gathered[base + i, 0], gathered[base + i, 1]
            top = pl.ds(i * wide, half_c)
            bottom = pl.ds(i * wide + half_c, half_c)
            weight[top, :nmu] = real
            weight[top, nmu:] = imag
            weight[bottom, :nmu] = -imag
            weight[bottom, nmu:] = real

    def forward(step):
        base = lax.rem(hi + high - step, high) * chunk
        fill(base)
        for group in range(2):
            for i in range(chunk):
                lanes = pl.ds(pl.multiple_of((base + i) * wide, 128), wide)
                data = b_recv[(base + i) * 2 + group].astype(F32).reshape(tall, wide)[:used]
                turned = swap_parts(data)
                block = fr[:, lanes][None] * data[:, None, :] + fi[:, lanes][None] * turned[:, None, :]
                left[:, i * wide : (i + 1) * wide] = block.reshape(used * points, wide).astype(BF16)
            part = jnp.dot(left[...], weight[...], preferred_element_type=F32)

            @pl.when(step == 0)
            def _():
                spec[group] = part

            @pl.when(step > 0)
            def _():
                spec[group] += part

    def arrive_and_use(s, carry):
        fourth(s, 0)
        fifth(s, 0)
        last(s - 1, 0)
        forward(s - 1)
        return carry

    lax.fori_loop(1, high, arrive_and_use, 0)
    last(high - 1, 0)
    forward(high - 1)
    load_s.wait()
    load_c.wait()

    def weigh(mu, carry):
        lanes = pl.ds(pl.multiple_of(mu * nmu, 128), nmu)
        sr, si = scr[0, :, lanes], scr[1, :, lanes]
        cr, ci = cpl[0, :, lanes], cpl[1, :, lanes]
        for j in range(vectors):
            at = pl.ds(pl.multiple_of(j * rows + mu * points, 16), points)
            fields = [(spec[g, at, :nmu], spec[g, at, nmu:]) for g in range(2)]
            for g in range(2):
                (ar, ai), (br, bi) = fields[g], fields[1 - g]
                real = sr * ar - si * ai + cr * br - ci * bi
                imag = sr * ai + si * ar + cr * bi + ci * br
                mixed[g, at, :nmu] = real.astype(BF16)
                mixed[g, at, nmu:] = (-imag).astype(BF16)
        return carry

    lax.fori_loop(0, share, weigh, 0)

    def backward(step, carry):
        base = lax.rem(step + 1 + hi, chunks) * chunk
        fill(base)
        for group in range(2):
            product = lax.dot_general(mixed[group], weight[...], nt, preferred_element_type=F32)
            for i in range(chunk):
                lanes = pl.ds(pl.multiple_of((base + i) * wide, 128), wide)
                block = product[:, i * wide : (i + 1) * wide].reshape(used, points, wide)
                plain = jnp.sum(fr[:, lanes][None] * block, axis=1)
                turned = jnp.sum(fi[:, lanes][None] * block, axis=1)
                result = (plain + swap_parts(turned)) * (1.0 / points)
                if used < tall:
                    result = jnp.concatenate([result, jnp.zeros((tall - used, wide), F32)], axis=0)
                t_send[(base + i) * 2 + group] = result.reshape(t_send.shape[1:]).astype(BF16)
        for group in range(2):
            for i in range(chunk):
                k = base + i
                here = (k == ka) & (group == grp)
                wanted = (group == grp) if split == 1 else (k >= 0)

                @pl.when(here)
                def _():
                    pltpu.make_async_copy(t_send.at[k * 2 + group], t_recv.at[place], t_sem).start()

                @pl.when(jnp.logical_not(here) & wanted)
                def _():
                    pltpu.make_async_remote_copy(
                        src_ref=t_send.at[k * 2 + group],
                        dst_ref=t_recv.at[place],
                        send_sem=t_send_sem,
                        recv_sem=t_sem,
                        device_id=(group, k),
                        device_id_type=MESH,
                    ).start()

        return carry

    lax.fori_loop(0, chunks, backward, 0)

    energy_v = levels_of(vidx_ref[...], vtab_ref[...])
    energy_c = levels_of(cidx_ref[...], ctab_ref[...])
    energy_c = jnp.sum(jnp.where(diagonal(half_c), energy_c, 0.0), axis=0, keepdims=True)
    energy = energy_c - energy_v
    group_sign = 1.0 - 2.0 * grp.astype(F32)

    pltpu.make_async_copy(t_recv, t_recv, t_sem).wait()
    blocks = t_recv[...].astype(F32).reshape(padded, wide).astype(BF16)
    products = jnp.dot(up[...], blocks, preferred_element_type=F32)
    for j in range(vectors):
        at = j * 2 * half_c
        d_real = products[at : at + half_c]
        d_imag = products[at + half_c : at + 2 * half_c]
        kern_real = d_real[:, :half_c] + d_imag[:, half_c:]
        kern_imag = d_imag[:, :half_c] - d_real[:, half_c:]
        for part, kern in enumerate((kern_real, kern_imag)):
            trial = amp_ref[0, 0, part, j].astype(F32)
            out_ref[0, 0, part, j] = (group_sign * (energy * trial - kern)).astype(BF16)

    sent = pl.ds(0, points - 1)
    pltpu.make_async_copy(gathered.at[sent], gathered.at[sent], c_send_sem).wait()
    sent = pl.ds(0, devices - 1)
    pltpu.make_async_copy(b_recv.at[sent], b_recv.at[sent], b_send_sem).wait()
    sent = pl.ds(0, slots - 1)
    pltpu.make_async_copy(t_recv.at[sent], t_recv.at[sent], t_send_sem).wait()


def body(
    amplitudes,
    valence_orbitals,
    conduction_orbitals,
    screened,
    coupling,
    grid_index,
    valence_index,
    conduction_index,
    valence_table,
    conduction_table,
):
    points = grid_index.shape[0]
    groups = lax.axis_size("grp")
    bands_c, nmu = conduction_orbitals.shape[2:]
    vectors = amplitudes.shape[3]
    wide = 2 * bands_c
    owned = screened.shape[2] // nmu
    split = groups if owned % groups == 0 else 1
    share = owned // split
    chunk = 4
    rows = share * points * vectors
    block = (-(-share * vectors // TILE), TILE, wide)
    vmem = pl.BlockSpec(memory_space=pltpu.VMEM)
    hbm = pl.BlockSpec(memory_space=pl.ANY)
    return pl.pallas_call(
        functools.partial(whole_kernel, split, share, chunk),
        out_shape=jax.ShapeDtypeStruct(amplitudes.shape, BF16),
        in_specs=[vmem] * 8 + [hbm] * 2,
        out_specs=vmem,
        scratch_shapes=[
            pltpu.VMEM((points, points * wide), F32),
            pltpu.VMEM((points, points * wide), F32),
            pltpu.VMEM((points, 2, bands_c, nmu), BF16),
            pltpu.VMEM((points * split,) + block, BF16),
            pltpu.VMEM((points * groups,) + block, BF16),
            pltpu.VMEM((points * groups,) + block, BF16),
            pltpu.VMEM((points * split,) + block, BF16),
            pltpu.VMEM((rows, chunk * wide), BF16),
            pltpu.VMEM((chunk * wide, 2 * nmu), BF16),
            pltpu.VMEM((groups, rows, 2 * nmu), F32),
            pltpu.VMEM((groups, rows, 2 * nmu), BF16),
            pltpu.VMEM((2, points, share * nmu), F32),
            pltpu.VMEM((2, points, share * nmu), F32),
            pltpu.VMEM((vectors * wide, points * split * block[0] * TILE), BF16),
            pltpu.SemaphoreType.DMA((2,)),
            pltpu.SemaphoreType.DMA,
            pltpu.SemaphoreType.DMA,
            pltpu.SemaphoreType.DMA((points, 2)),
            pltpu.SemaphoreType.DMA,
            pltpu.SemaphoreType.DMA,
            pltpu.SemaphoreType.DMA,
            pltpu.SemaphoreType.DMA,
        ],
        compiler_params=pltpu.CompilerParams(
            collective_id=0, has_side_effects=True, vmem_limit_bytes=60 * 2**20
        ),
    )(
        amplitudes,
        valence_orbitals,
        conduction_orbitals,
        grid_index[None],
        valence_index,
        conduction_index,
        valence_table[None],
        conduction_table[None],
        screened,
        coupling,
    )


def solution(mesh):
    placed = (
        P("grp", "ka", None, None, None, None),
        P("ka", None, None, None),
        P("ka", None, None, None),
        P(None, None, "ka"),
        P(None, None, "ka"),
        P(),
        P("ka", None),
        P("ka", None),
        P(),
        P(),
    )
    return jax.shard_map(
        body,
        mesh=mesh,
        in_specs=placed,
        out_specs=P("grp", "ka", None, None, None, None),
        check_vma=False,
    )
```
